128 devices in a mesh: row: 8 (over z, x_hi), col: 16 (over y, x_lo, core).
Axes of the slice: x: 4 (x_hi: 2, x_lo: 2; x = x_hi * 2 + x_lo), y: 4, z: 4, core: 2. Of those that a mesh axis runs over, the one named last changes fastest.
Arguments:
- tokens: bfloat16 [512, 4096], P(('row', 'col')), may hold values from -24 to 24
- counts: int32 [128], P(('row', 'col')), may hold values from 1 to 4, 416 in all
- cotangent: bfloat16 [512, 4096], P(('row', 'col')), may hold values from -6 to 6
- up_weight: bfloat16 [2, 4096, 16384], P(None, 'col', 'row'), may hold values from -0.09375 to 0.09375
- down_weight: bfloat16 [2, 16384, 4096], P(None, 'row', 'col'), may hold values from -0.046875 to 0.046875
- norm_gain: float32 [2, 4096], P(None, 'col'), may hold values from 0.5 to 2
Outputs:
- token_grad: bfloat16 [512, 4096], P(('row', 'col'))
- up_grad: float32 [2, 4096, 16384], P(None, 'col', 'row')
- down_grad: float32 [2, 16384, 4096], P(None, 'row', 'col')
- gain_grad: float32 [2, 4096], P(None, 'col')
The draws below stay inside these ranges and needn't reach their ends.
All inputs are finite; a program needn't handle non-finite values. No bound on the sum of `counts` on one device may be relied on, other than what follows from the above.
Results may differ from the reference program's by a relative error of at most 0.0095.
Values may be sent and summed in bfloat16 or wider, within the bound.
No kernel may reach another device: no remote copies, remote signals or barrier semaphores. Data moves between devices by JAX's collectives and lax.ppermute only.
A program may use at most 128 MiB of HBM per device.

```python
import math
import jax
import jax.numpy as jnp
import numpy as np
from jax import lax

D = 4096
FF = 16384
LAYERS = 2
SLOTS = 4
TILES = 128
TOKENS = 512


def draw_tokens(key, part):
    key_noise, key_rows = jax.random.split(key, 2)
    columns = jnp.arange(D, dtype=jnp.float32) / D
    column_scale = jnp.exp(jnp.log(0.4) + jnp.log(10.0) * columns)[None, :]
    noise_part = jnp.clip(jax.random.normal(key_noise, (TOKENS, D), jnp.float32), -6.0, 6.0)
    row_scale = jnp.exp(jax.random.uniform(key_rows, (TOKENS, 1), jnp.float32, jnp.log(0.1), jnp.log(1.0)))
    values = noise_part * row_scale * column_scale
    return values.astype(jnp.bfloat16)


def shard_levels(own_key, extent, cuts, low, top_value):
    def one(axis_at, parts):
        draws = jax.random.uniform(jax.random.fold_in(jax.random.fold_in(own_key, 6), axis_at), (parts,), jnp.float32, low / len(cuts), top_value / len(cuts))
        return jnp.repeat(jnp.exp(draws), extent[axis_at] // parts).reshape((-1,) + (1,) * (len(extent) - axis_at - 1))

    level = one(*cuts[0])
    for cut in cuts[1:]:
        level = level * one(*cut)
    return level


def split_up(number_of, total, reach, slope):
    weights = [(1 << 20) // math.isqrt(grade ** slope) + 1 for grade in range(2, number_of + 1)]
    surplus, holding = total - reach - (number_of - 1), [1] * (number_of - 1)
    while surplus > 0:
        candidates = [i for i in range(number_of - 1) if holding[i] < reach]
        pool, remaining = sum([weights[i] for i in candidates]), surplus
        for i in candidates:
            extra = min(reach - holding[i], max(1, remaining * weights[i] // pool), surplus)
            holding[i] = holding[i] + extra
            surplus = surplus - extra
    return np.array([reach] + holding)


def ragged(stream_key, count, total, limit, lean):
    if count == 2:
        one = jax.random.randint(stream_key, (), max(1, total - limit), min(limit, total - 1) + 1)
        return jnp.stack([one, total - one])
    lengths = jnp.asarray(split_up(count, total, limit, lean), jnp.int32)
    twos = (count - 1) // 2
    giver, sink = lengths[1:1 + 2 * twos:2], lengths[2:2 + 2 * twos:2]
    margin = jnp.minimum(giver - 1, limit - sink)
    passed = jax.random.randint(jax.random.fold_in(stream_key, 1), (twos,), 0, 1 << 20) % (margin + 1)
    lengths = lengths.at[1:1 + 2 * twos:2].set(giver - passed).at[2:2 + 2 * twos:2].set(sink + passed)
    return lengths[jax.random.permutation(jax.random.fold_in(stream_key, 2), count)]


def normal_values(rng, shape, scale, limit, cuts=(), held_as=jnp.bfloat16):
    entries = jax.random.normal(rng, shape, jnp.float32) * scale
    if len(cuts) > 0:
        entries = shard_levels(rng, shape, cuts, -0.22, 0.18) * entries
    return jnp.clip(entries, min=-limit, max=limit).astype(held_as)


def setup_inputs(seed: int = 0) -> dict:
    key_list = jax.random.split(jax.random.key(seed), 7)
    tokens = draw_tokens(jax.random.fold_in(key_list[6], 71), 0)
    counts = ragged(key_list[1], TILES, TILES * SLOTS - (TILES // 4) * (SLOTS - 1), SLOTS, 1).astype(jnp.int32)
    cotangent = normal_values(key_list[2], (TOKENS, D), 1.0, 6.0, ((0, 128),))
    up_weight = normal_values(key_list[3], (LAYERS, D, FF), D ** -0.5, 0.09375, ((1, 16), (2, 8)))
    down_weight = normal_values(key_list[4], (LAYERS, FF, D), FF ** -0.5, 0.046875, ((1, 8), (2, 16)))
    norm_gain = jnp.clip(jnp.exp(math.log(2.0) - 1.3862944 * jax.random.uniform(key_list[5], (LAYERS, D), jnp.float32) ** shard_levels(key_list[5], (LAYERS, D), ((1, 16),), -0.2, 0.2)), 0.5, 2.0)
    return {"tokens": tokens, "counts": counts, "cotangent": cotangent, "up_weight": up_weight, "down_weight": down_weight, "norm_gain": norm_gain}


epsilon_norm = 1e-06
gelu_scale = 0.7978845608028654
cubic_term = 0.044715

def gelu_value(pre_act):
    tangent = jnp.tanh(gelu_scale * (pre_act + cubic_term * pre_act * pre_act * pre_act))
    return 0.5 * pre_act * (1.0 + tangent)

def gelu_slope(pre_act):
    tangent = jnp.tanh(gelu_scale * (pre_act + cubic_term * pre_act * pre_act * pre_act))
    return 0.5 * (1.0 + tangent) + 0.5 * pre_act * (1.0 - tangent * tangent) * gelu_scale * (1.0 + 3.0 * cubic_term * pre_act * pre_act)

def reference(tokens, counts, cotangent, up_weight, down_weight, norm_gain):
    positions = jnp.arange(TOKENS, dtype=jnp.int32)
    live_rows = (positions % SLOTS < counts[positions // SLOTS]).astype(jnp.float32)[:, None]
    stream = tokens.astype(jnp.float32)
    saved = []
    for layer_index in range(LAYERS):
        scale_rows = lax.rsqrt(lax.optimization_barrier(jnp.mean(stream * stream, axis=1, keepdims=True)) + epsilon_norm)
        normed = (stream * scale_rows * norm_gain[layer_index][None, :]).astype(jnp.bfloat16)
        pre_act = jnp.dot(normed, up_weight[layer_index], preferred_element_type=jnp.float32)
        hidden = gelu_value(pre_act).astype(jnp.bfloat16)
        saved.append((stream, scale_rows, normed, hidden, pre_act))
        stream = stream + jnp.dot(hidden, down_weight[layer_index], preferred_element_type=jnp.float32)
    grad_stream = cotangent.astype(jnp.float32) * live_rows
    up_grads = []
    down_grads = []
    gain_grads = []
    for layer_index in reversed(range(LAYERS)):
        stream_in, scale_rows, normed, hidden, pre_act = saved[layer_index]
        grad_bf = grad_stream.astype(jnp.bfloat16)
        down_grads.append(jnp.dot(hidden.T, grad_bf, preferred_element_type=jnp.float32))
        grad_hidden = jnp.dot(grad_bf, down_weight[layer_index].T, preferred_element_type=jnp.float32)
        grad_pre = (grad_hidden * gelu_slope(pre_act)).astype(jnp.bfloat16)
        up_grads.append(jnp.dot(normed.T, grad_pre, preferred_element_type=jnp.float32))
        grad_normed = jnp.dot(grad_pre, up_weight[layer_index].T, preferred_element_type=jnp.float32)
        unit_rows = stream_in * scale_rows
        gain_grads.append(lax.optimization_barrier(jnp.sum(grad_normed * unit_rows, axis=0)))
        weighted = grad_normed * norm_gain[layer_index][None, :]
        inner_mean = lax.optimization_barrier(jnp.mean(weighted * unit_rows, axis=1, keepdims=True))
        grad_stream = grad_stream + scale_rows * (weighted - unit_rows * inner_mean)
    token_grad = grad_stream.astype(jnp.bfloat16)
    return (token_grad, jnp.stack(up_grads[::-1]), jnp.stack(down_grads[::-1]), jnp.stack(gain_grads[::-1]))
```

```python
import jax
import jax.numpy as jnp
from jax import lax
from jax.sharding import PartitionSpec as P

D = 4096
F32 = jnp.float32
BF16 = jnp.bfloat16

epsilon_norm = 1e-06
gelu_scale = 0.7978845608028654
cubic_term = 0.044715
contract_rows = (((0,), (0,)), ((), ()))
contract_cols = (((1,), (1,)), ((), ()))

LIVE_PER_CHUNK = 52
CHUNK = 56
CHUNKS = 8
ROWS = CHUNK * CHUNKS
SIDE = LIVE_PER_CHUNK
DEAD = 1e30


chip_groups = [[2 * chip + core for chip in range(8)] for core in range(2)]
core_pairs = [(i, i ^ 1) for i in range(16)]


def swap_cores(value):
    return lax.ppermute(value, "col", core_pairs)


def exchange(blocks, axis):
    groups = chip_groups if axis == "col" else None
    return lax.all_to_all(blocks, axis, split_axis=0, concat_axis=0, tiled=True, axis_index_groups=groups)


def reduce_scatter(blocks, axis):
    return jnp.sum(exchange(blocks.astype(BF16), axis).astype(F32), axis=0)


def all_gather(block, axis):
    return exchange(jnp.broadcast_to(block[None], (CHUNKS,) + block.shape), axis)


def gelu_both(pre):
    tangent = jnp.tanh(gelu_scale * (pre + cubic_term * pre * pre * pre))
    value = 0.5 * pre * (1.0 + tangent)
    slope = 0.5 * (1.0 + tangent) + 0.5 * pre * (1.0 - tangent * tangent) * gelu_scale * (
        1.0 + 3.0 * cubic_term * pre * pre
    )
    return value, slope


def dot(a, b):
    return jnp.dot(a, b, preferred_element_type=F32)


def to_row(column):
    n = column.shape[0]
    return jnp.sum(jnp.where(jnp.eye(n, dtype=bool), column, 0.0), axis=0, keepdims=True)


def to_column(row):
    n = row.shape[1]
    return jnp.sum(jnp.where(jnp.eye(n, dtype=bool), row, 0.0), axis=1, keepdims=True)


def pad_row(row, width):
    return jnp.pad(row, ((0, 0), (0, width - row.shape[1])))


def put_side(chunks, row):
    at = lax.broadcasted_iota(jnp.int32, (1, chunks.shape[1], 1), 1)
    last = SIDE if chunks.shape[1] == CHUNK else chunks.shape[1] - 8
    return jnp.where(at == last, row[None], jnp.where(at > last, 0.0, chunks))


def on_device(tokens, counts, cotangent, up_weight, down_weight, norm_gain):
    row = lax.axis_index("row")
    core = lax.axis_index("col") % 2
    chip = lax.axis_index("col") // 2

    up_blocks, down_blocks, gains = [], [], []
    gain_other = swap_cores(norm_gain)
    for layer in range(2):
        keep = lax.dynamic_slice_in_dim(up_weight[layer], core * 1024, 1024, 1)
        give = lax.dynamic_slice_in_dim(up_weight[layer], (1 - core) * 1024, 1024, 1)
        up_blocks.append(jnp.concatenate([keep, swap_cores(give)], axis=0))
        keep = lax.dynamic_slice_in_dim(down_weight[layer], core * 1024, 1024, 0)
        give = lax.dynamic_slice_in_dim(down_weight[layer], (1 - core) * 1024, 1024, 0)
        down_blocks.append(jnp.concatenate([keep, swap_cores(give)], axis=1))
        gains.append(jnp.concatenate([norm_gain[layer], gain_other[layer]])[None, :])

    live = (jnp.arange(4, dtype=jnp.int32) < counts[0])[:, None]
    mixed = jnp.concatenate(
        [jnp.where(live, tokens, jnp.asarray(DEAD, BF16)), jnp.where(live, cotangent, jnp.asarray(0, BF16))], axis=0
    )
    mixed = mixed.reshape(8, 16, 256).transpose(1, 0, 2)
    mixed = lax.all_to_all(mixed, "col", split_axis=0, concat_axis=0, tiled=True)
    mixed = all_gather(mixed.reshape(128, 256), "row").reshape(1024, 256)

    pick = (lax.broadcasted_iota(jnp.int32, (8, 256), 1) == 0).astype(BF16)
    marks = lax.dot_general(pick, mixed, contract_cols, preferred_element_type=F32)[:1]
    lane = lax.broadcasted_iota(jnp.int32, (1, 1024), 1)
    alive = (marks < 1e20) & (lane % 8 < 4)
    before = lax.broadcasted_iota(jnp.int32, (1024, 1024), 0) < lax.broadcasted_iota(jnp.int32, (1024, 1024), 1)
    place = dot(jnp.broadcast_to(alive, (8, 1024)).astype(BF16), before.astype(BF16))[:1].astype(jnp.int32)
    place = place + (CHUNK - LIVE_PER_CHUNK) * (place // LIVE_PER_CHUNK)
    place = jnp.where(alive, place, -1)
    slots = lax.broadcasted_iota(jnp.int32, (ROWS, 1024), 0)
    stream_own = dot((slots == place).astype(BF16), mixed).astype(BF16)
    place_grad = jnp.where(lane % 8 < 4, -1, jnp.roll(place, 4, axis=1))
    grad_own = dot((slots == place_grad).astype(BF16), mixed).astype(BF16)
    place_token = place.reshape(128, 8)[:, :4].reshape(512, 1)

    def rows_of(chunk_index):
        at = lax.broadcasted_iota(jnp.int32, (CHUNK, ROWS), 0) + chunk_index * CHUNK
        return at == lax.broadcasted_iota(jnp.int32, (CHUNK, ROWS), 1)

    own_rows = rows_of(chip)
    real_row = lax.broadcasted_iota(jnp.int32, (CHUNK, 1), 0) < LIVE_PER_CHUNK
    real_all = lax.broadcasted_iota(jnp.int32, (ROWS, 1), 0) % CHUNK < LIVE_PER_CHUNK

    def both(own):
        return jnp.concatenate([own, swap_cores(own)], axis=1)

    def hidden_grad(grad_pair, layer):
        part = lax.dot_general(grad_pair, down_blocks[layer], contract_cols, preferred_element_type=F32)
        return reduce_scatter(part.reshape(CHUNKS, CHUNK, 1024), "col")

    def fold_cores(pair):
        return pair[:, :256] + swap_cores(pair[:, 256:].astype(BF16)).astype(F32)

    grad_pair = both(grad_own)
    stream_pair = both(stream_own)
    stream_f32 = lax.dynamic_slice_in_dim(stream_own, row * CHUNK, CHUNK, 0).astype(F32)
    grad_f32 = lax.dynamic_slice_in_dim(grad_own, row * CHUNK, CHUNK, 0).astype(F32)

    saved = []
    for layer in range(2):
        scaled = (stream_pair.astype(F32) * gains[layer]).astype(BF16)
        squares = jnp.sum(jnp.square(stream_pair.astype(F32)), axis=1, keepdims=True)
        part = dot(scaled, up_blocks[layer]).reshape(CHUNKS, CHUNK, 1024)
        part = put_side(part, pad_row(to_row(squares), 1024))
        summed = reduce_scatter(part, "col")
        rstd = lax.rsqrt(summed[SIDE : SIDE + 1, :ROWS] / D + epsilon_norm)
        rstd_rows = jnp.sum(jnp.where(own_rows, rstd, 0.0), axis=1, keepdims=True)
        pre = jnp.where(real_row, summed * rstd_rows, 0.0)
        value, slope = gelu_both(pre)
        hidden = all_gather(value.astype(BF16), "col").reshape(ROWS, 1024)
        saved.append((stream_own, stream_pair, to_column(rstd), pre, slope, hidden))
        if layer == 0:
            moved = fold_cores(dot(hidden, down_blocks[0])).reshape(CHUNKS, CHUNK, 256)
            stream_f32 = stream_f32 + reduce_scatter(moved, "row")
            stream_own = all_gather(stream_f32.astype(BF16), "row").reshape(ROWS, 256)
            stream_pair = both(stream_own)

    up_grads, down_grads, gain_grads = [None, None], [None, None], [None, None]
    for layer in (1, 0):
        stream_own, stream_pair, rstd, pre, slope, hidden = saved[layer]
        grad_hidden = hidden_grad(grad_pair, layer)
        grad_pre = (grad_hidden * slope).astype(BF16)
        inner = jnp.sum(grad_pre.astype(F32) * pre, axis=1, keepdims=True)
        inner = jnp.sum(jnp.where(own_rows, inner, 0.0), axis=0, keepdims=True)
        at = lax.broadcasted_iota(jnp.int32, (CHUNK, 1), 0)
        grad_pre = jnp.where(at == SIDE, pad_row(inner, 1024).astype(BF16), grad_pre)
        grad_pre = all_gather(grad_pre, "col")
        inner = to_column(jnp.sum(grad_pre[:, SIDE, :ROWS].astype(F32), axis=0, keepdims=True))
        grad_pre = grad_pre.reshape(ROWS, 1024)
        grad_normed = lax.dot_general(grad_pre, up_blocks[layer], contract_cols, preferred_element_type=F32)
        unit = stream_pair.astype(F32) * rstd
        gain_part = jnp.sum(jnp.where(real_all, grad_normed * unit, 0.0), axis=0, keepdims=True)
        change = jnp.where(real_all, rstd * (grad_normed * gains[layer] - unit * (inner / D)), 0.0)
        change = put_side(change.reshape(CHUNKS, CHUNK, 512), gain_part).reshape(ROWS, 512)
        change = fold_cores(change)
        gain_part = change[SIDE : SIDE + 1]

        grad_pre_other = swap_cores(grad_pre)
        hidden_other = swap_cores(hidden)
        first = core == 0
        unit_own = jnp.where(real_all, stream_own.astype(F32) * rstd * norm_gain[layer][None, :], 0.0).astype(BF16)
        pair = jnp.concatenate(
            [jnp.where(first, grad_pre, grad_pre_other), jnp.where(first, grad_pre_other, grad_pre)], axis=1
        )
        up_grads[layer] = lax.dot_general(unit_own, pair, contract_rows, preferred_element_type=F32)
        pair = jnp.concatenate([jnp.where(first, hidden, hidden_other), jnp.where(first, hidden_other, hidden)], axis=1)
        down_grads[layer] = lax.dot_general(pair, grad_own, contract_rows, preferred_element_type=F32)

        if layer == 1:
            summed = reduce_scatter(change.reshape(CHUNKS, CHUNK, 256), "row")
            gain_grads[1] = summed[SIDE]
            grad_f32 = jnp.where(real_row, grad_f32 + summed, 0.0)
            grad_own = all_gather(grad_f32.astype(BF16), "row").reshape(ROWS, 256)
            grad_pair = both(grad_own)
        else:
            mine = (jnp.arange(CHUNKS) == row)[:, None, None]
            change = change.reshape(CHUNKS, CHUNK, 256) + jnp.where(mine, grad_f32[None], 0.0)
            change = change.reshape(ROWS, 256).astype(BF16)
            back = (place_token == lax.broadcasted_iota(jnp.int32, (512, ROWS), 1)).astype(BF16)
            spread = dot(back, change).reshape(8, 64, 256)
            spread = jnp.concatenate([spread, jnp.broadcast_to(gain_part[None], (8, 8, 256))], axis=1)
            summed = reduce_scatter(spread, "row")
            gain_grads[0] = summed[64]
            token_grad = summed[:64].astype(BF16).reshape(16, 4, 256)
            token_grad = lax.all_to_all(token_grad, "col", split_axis=0, concat_axis=0, tiled=True)
            token_grad = token_grad.transpose(1, 0, 2).reshape(4, 4096)
    return token_grad, jnp.stack(up_grads), jnp.stack(down_grads), jnp.stack(gain_grads)


def solution(mesh):
    placed = (
        P(("row", "col"), None),
        P(("row", "col")),
        P(("row", "col"), None),
        P(None, "col", "row"),
        P(None, "row", "col"),
        P(None, "col"),
    )
    return jax.shard_map(
        on_device,
        mesh=mesh,
        in_specs=placed,
        out_specs=(
            P(("row", "col"), None),
            P(None, "col", "row"),
            P(None, "row", "col"),
            P(None, "col"),
        ),
        check_vma=False,
    )
```

```python
import jax
import jax.numpy as jnp
from jax import lax
from jax.sharding import PartitionSpec as P


D = 4096
F32 = jnp.float32
BF16 = jnp.bfloat16

epsilon_norm = 1e-06
gelu_scale = 0.7978845608028654
cubic_term = 0.044715
contract_rows = (((0,), (0,)), ((), ()))
contract_cols = (((1,), (1,)), ((), ()))

LIVE_PER_CHUNK = 52
CHUNK = 56
CHUNKS = 8
ROWS = CHUNK * CHUNKS
SIDE = LIVE_PER_CHUNK
DEAD = 1e30


chip_groups = [[2 * chip + core for chip in range(8)] for core in range(2)]
core_pairs = [(i, i ^ 1) for i in range(16)]


def swap_cores(value):
    return lax.ppermute(value, "col", core_pairs)


def exchange(blocks, axis):
    groups = chip_groups if axis == "col" else None
    return lax.all_to_all(blocks, axis, split_axis=0, concat_axis=0, tiled=True, axis_index_groups=groups)


def reduce_scatter(blocks, axis):
    return jnp.sum(exchange(blocks.astype(BF16), axis).astype(F32), axis=0)


def all_gather(block, axis):
    return exchange(jnp.broadcast_to(block[None], (CHUNKS,) + block.shape), axis)


def chip_permute(value, bits):
    return lax.ppermute(value, "col", [(i, i ^ (2 * bits)) for i in range(16)])


def quiet_reduce_scatter(blocks, chip):
    far, near = chip // 2, chip % 2
    blocks = blocks.reshape((4, 2) + blocks.shape[1:])
    got = [
        chip_permute(lax.dynamic_index_in_dim(blocks, far ^ k, 0, keepdims=False).astype(BF16), 2 * k)
        for k in (1, 3, 2)
    ]
    total = lax.dynamic_index_in_dim(blocks, far, 0, keepdims=False)
    for value in got:
        total = total + value.astype(F32)
    got = chip_permute(lax.dynamic_index_in_dim(total, 1 - near, 0, keepdims=False).astype(BF16), 1)
    return lax.dynamic_index_in_dim(total, near, 0, keepdims=False) + got.astype(F32)


def quiet_all_gather(block, chip):
    far, near = chip // 2, chip % 2
    other = chip_permute(block, 1)
    pair = jnp.stack([jnp.where(near == 0, block, other), jnp.where(near == 0, other, block)])
    pairs = [pair] + [chip_permute(pair, 2 * k) for k in (1, 2, 3)]
    out = jnp.zeros((4,) + pair.shape, pair.dtype)
    for k in range(4):
        out = lax.dynamic_update_index_in_dim(out, pairs[k], far ^ k, 0)
    return out.reshape((8,) + block.shape)


def gelu_both(pre):
    tangent = jnp.tanh(gelu_scale * (pre + cubic_term * pre * pre * pre))
    value = 0.5 * pre * (1.0 + tangent)
    slope = 0.5 * (1.0 + tangent) + 0.5 * pre * (1.0 - tangent * tangent) * gelu_scale * (
        1.0 + 3.0 * cubic_term * pre * pre
    )
    return value, slope


def dot(a, b):
    return jnp.dot(a, b, preferred_element_type=F32)


def to_row(column):
    n = column.shape[0]
    return jnp.sum(jnp.where(jnp.eye(n, dtype=bool), column, 0.0), axis=0, keepdims=True)


def to_column(row):
    n = row.shape[1]
    return jnp.sum(jnp.where(jnp.eye(n, dtype=bool), row, 0.0), axis=1, keepdims=True)


def pad_row(row, width):
    return jnp.pad(row, ((0, 0), (0, width - row.shape[1])))


def put_side(chunks, row):
    at = lax.broadcasted_iota(jnp.int32, (1, chunks.shape[1], 1), 1)
    last = SIDE if chunks.shape[1] == CHUNK else chunks.shape[1] - 8
    return jnp.where(at == last, row[None], jnp.where(at > last, 0.0, chunks))


def whole(tokens, counts, cotangent, up_weight, down_weight, norm_gain):
    row = lax.axis_index("row")
    core = lax.axis_index("col") % 2
    chip = lax.axis_index("col") // 2

    up_blocks, down_blocks, gains = [], [], []
    gain_other = swap_cores(norm_gain)
    for layer in range(2):
        keep = lax.dynamic_slice_in_dim(up_weight[layer], core * 1024, 1024, 1)
        give = lax.dynamic_slice_in_dim(up_weight[layer], (1 - core) * 1024, 1024, 1)
        up_blocks.append(jnp.concatenate([keep, swap_cores(give)], axis=0))
        keep = lax.dynamic_slice_in_dim(down_weight[layer], core * 1024, 1024, 0)
        give = lax.dynamic_slice_in_dim(down_weight[layer], (1 - core) * 1024, 1024, 0)
        down_blocks.append(jnp.concatenate([keep, swap_cores(give)], axis=1))
        gains.append(jnp.concatenate([norm_gain[layer], gain_other[layer]])[None, :])

    live = (jnp.arange(4, dtype=jnp.int32) < counts[0])[:, None]
    mixed = jnp.concatenate(
        [jnp.where(live, tokens, jnp.asarray(DEAD, BF16)), jnp.where(live, cotangent, jnp.asarray(0, BF16))], axis=0
    )
    mixed = mixed.reshape(8, 16, 256).transpose(1, 0, 2)
    mixed = jnp.broadcast_to(mixed[None], (8, 16, 8, 256)).reshape(128, 8, 256)
    mixed = lax.all_to_all(mixed, ("row", "col"), split_axis=0, concat_axis=0, tiled=True).reshape(1024, 256)

    pick = (lax.broadcasted_iota(jnp.int32, (8, 256), 1) == 0).astype(BF16)
    marks = lax.dot_general(pick, mixed, contract_cols, preferred_element_type=F32)[:1]
    lane = lax.broadcasted_iota(jnp.int32, (1, 1024), 1)
    alive = (marks < 1e20) & (lane % 8 < 4)
    before = lax.broadcasted_iota(jnp.int32, (1024, 1024), 0) < lax.broadcasted_iota(jnp.int32, (1024, 1024), 1)
    place = dot(jnp.broadcast_to(alive, (8, 1024)).astype(BF16), before.astype(BF16))[:1].astype(jnp.int32)
    place = place + (CHUNK - LIVE_PER_CHUNK) * (place // LIVE_PER_CHUNK)
    place = jnp.where(alive, place, -1)
    slots = lax.broadcasted_iota(jnp.int32, (ROWS, 1024), 0)
    stream_own = dot((slots == place).astype(BF16), mixed).astype(BF16)
    place_grad = jnp.where(lane % 8 < 4, -1, jnp.roll(place, 4, axis=1))
    grad_own = dot((slots == place_grad).astype(BF16), mixed).astype(BF16)
    place_token = place.reshape(128, 8)[:, :4].reshape(512, 1)

    def rows_of(chunk_index):
        at = lax.broadcasted_iota(jnp.int32, (CHUNK, ROWS), 0) + chunk_index * CHUNK
        return at == lax.broadcasted_iota(jnp.int32, (CHUNK, ROWS), 1)

    own_rows = rows_of(chip)
    real_row = lax.broadcasted_iota(jnp.int32, (CHUNK, 1), 0) < LIVE_PER_CHUNK
    real_all = lax.broadcasted_iota(jnp.int32, (ROWS, 1), 0) % CHUNK < LIVE_PER_CHUNK

    def both(own):
        return jnp.concatenate([own, swap_cores(own)], axis=1)

    def hidden_grad(grad_pair, layer):
        part = lax.dot_general(grad_pair, down_blocks[layer], contract_cols, preferred_element_type=F32)
        part = part.reshape(CHUNKS, CHUNK, 1024)
        if layer == 1:
            return quiet_reduce_scatter(part, chip)
        return reduce_scatter(part, "col")

    def fold_cores(pair):
        return pair[:, :256] + swap_cores(pair[:, 256:].astype(BF16)).astype(F32)

    grad_pair = both(grad_own)
    stream_pair = both(stream_own)
    stream_f32 = lax.dynamic_slice_in_dim(stream_own, row * CHUNK, CHUNK, 0).astype(F32)
    grad_f32 = lax.dynamic_slice_in_dim(grad_own, row * CHUNK, CHUNK, 0).astype(F32)

    saved = []
    for layer in range(2):
        scaled = (stream_pair.astype(F32) * gains[layer]).astype(BF16)
        squares = jnp.sum(jnp.square(stream_pair.astype(F32)), axis=1, keepdims=True)
        part = dot(scaled, up_blocks[layer]).reshape(CHUNKS, CHUNK, 1024)
        part = put_side(part, pad_row(to_row(squares), 1024))
        summed = reduce_scatter(part, "col")
        rstd = lax.rsqrt(summed[SIDE : SIDE + 1, :ROWS] / D + epsilon_norm)
        rstd_rows = jnp.sum(jnp.where(own_rows, rstd, 0.0), axis=1, keepdims=True)
        pre = jnp.where(real_row, summed * rstd_rows, 0.0)
        value, slope = gelu_both(pre)
        if layer == 0:
            hidden = all_gather(value.astype(BF16), "col").reshape(ROWS, 1024)
        else:
            hidden = quiet_all_gather(value.astype(BF16), chip).reshape(ROWS, 1024)
        saved.append((stream_own, stream_pair, to_column(rstd), pre, slope, hidden))
        if layer == 0:
            moved = fold_cores(dot(hidden, down_blocks[0])).reshape(CHUNKS, CHUNK, 256)
            stream_f32 = stream_f32 + reduce_scatter(moved, "row")
            stream_own = all_gather(stream_f32.astype(BF16), "row").reshape(ROWS, 256)
            stream_pair = both(stream_own)

    up_grads, down_grads, gain_grads = [None, None], [None, None], [None, None]
    for layer in (1, 0):
        stream_own, stream_pair, rstd, pre, slope, hidden = saved[layer]
        grad_hidden = hidden_grad(grad_pair, layer)
        grad_pre = (grad_hidden * slope).astype(BF16)
        inner = jnp.sum(grad_pre.astype(F32) * pre, axis=1, keepdims=True)
        inner = jnp.sum(jnp.where(own_rows, inner, 0.0), axis=0, keepdims=True)
        at = lax.broadcasted_iota(jnp.int32, (CHUNK, 1), 0)
        grad_pre = jnp.where(at == SIDE, pad_row(inner, 1024).astype(BF16), grad_pre)
        grad_pre = all_gather(grad_pre, "col")
        inner = to_column(jnp.sum(grad_pre[:, SIDE, :ROWS].astype(F32), axis=0, keepdims=True))
        grad_pre = grad_pre.reshape(ROWS, 1024)
        grad_normed = lax.dot_general(grad_pre, up_blocks[layer], contract_cols, preferred_element_type=F32)
        unit = stream_pair.astype(F32) * rstd
        gain_part = jnp.sum(jnp.where(real_all, grad_normed * unit, 0.0), axis=0, keepdims=True)
        change = jnp.where(real_all, rstd * (grad_normed * gains[layer] - unit * (inner / D)), 0.0)
        change = put_side(change.reshape(CHUNKS, CHUNK, 512), gain_part).reshape(ROWS, 512)
        change = fold_cores(change)
        gain_part = change[SIDE : SIDE + 1]

        grad_pre_other = swap_cores(grad_pre)
        hidden_other = swap_cores(hidden)
        first = core == 0
        unit_own = jnp.where(real_all, stream_own.astype(F32) * rstd * norm_gain[layer][None, :], 0.0).astype(BF16)
        pair = jnp.concatenate(
            [jnp.where(first, grad_pre, grad_pre_other), jnp.where(first, grad_pre_other, grad_pre)], axis=1
        )
        up_grads[layer] = lax.dot_general(unit_own, pair, contract_rows, preferred_element_type=F32)
        pair = jnp.concatenate([jnp.where(first, hidden, hidden_other), jnp.where(first, hidden_other, hidden)], axis=1)
        down_grads[layer] = lax.dot_general(pair, grad_own, contract_rows, preferred_element_type=F32)

        if layer == 1:
            summed = reduce_scatter(change.reshape(CHUNKS, CHUNK, 256), "row")
            gain_grads[1] = summed[SIDE]
            grad_f32 = jnp.where(real_row, grad_f32 + summed, 0.0)
            grad_own = all_gather(grad_f32.astype(BF16), "row").reshape(ROWS, 256)
            grad_pair = both(grad_own)
        else:
            mine = (jnp.arange(CHUNKS) == row)[:, None, None]
            change = change.reshape(CHUNKS, CHUNK, 256) + jnp.where(mine, grad_f32[None], 0.0)
            change = change.reshape(ROWS, 256).astype(BF16)
            back = (place_token == lax.broadcasted_iota(jnp.int32, (512, ROWS), 1)).astype(BF16)
            spread = dot(back, change).reshape(128, 4, 256)
            spread = jnp.concatenate([spread, jnp.broadcast_to(gain_part[None], (128, 4, 256))], axis=1)
            spread = lax.all_to_all(spread.astype(BF16), ("row", "col"), split_axis=0, concat_axis=0, tiled=True)
            summed = jnp.sum(spread.reshape(8, 16, 8, 256).astype(F32), axis=0)
            gain_grads[0] = lax.dynamic_index_in_dim(summed, lax.axis_index("col"), 0, keepdims=False)[4]
            token_grad = summed[:, :4].astype(BF16).transpose(1, 0, 2).reshape(4, 4096)
    return token_grad, jnp.stack(up_grads), jnp.stack(down_grads), jnp.stack(gain_grads)


def solution(mesh):
    placed = (
        P(("row", "col"), None),
        P(("row", "col")),
        P(("row", "col"), None),
        P(None, "col", "row"),
        P(None, "row", "col"),
        P(None, "col"),
    )
    return jax.shard_map(
        whole,
        mesh=mesh,
        in_specs=placed,
        out_specs=(
            P(("row", "col"), None),
            P(None, "col", "row"),
            P(None, "row", "col"),
            P(None, "col"),
        ),
        check_vma=False,
    )
```

```python
import jax
import jax.numpy as jnp
from jax import lax
from jax.experimental import pallas as pl
from jax.experimental.pallas import tpu as pltpu
from jax.sharding import PartitionSpec as P


D = 4096
F32 = jnp.float32
BF16 = jnp.bfloat16

epsilon_norm = 1e-06
gelu_scale = 0.7978845608028654
cubic_term = 0.044715
contract_rows = (((0,), (0,)), ((), ()))
contract_cols = (((1,), (1,)), ((), ()))

LIVE_PER_CHUNK = 52
CHUNK = 56
CHUNKS = 8
ROWS = CHUNK * CHUNKS
SIDE = LIVE_PER_CHUNK
DEAD = 1e30


def swap_cores(value):
    return lax.ppermute(value, "col", [(i, i ^ 1) for i in range(16)])


def chip_permute(value, bits):
    return lax.ppermute(value, "col", [(i, i ^ (2 * bits)) for i in range(16)])


def row_permute(value, bits):
    return lax.ppermute(value, "row", [(i, i ^ bits) for i in range(8)])


def reduce_scatter(part):
    blocks = part.reshape(4, 2 * CHUNK, part.shape[1])
    got = [chip_permute(blocks[k].astype(BF16), 2 * k) for k in (1, 3, 2)]
    total = blocks[0]
    for value in got:
        total = total + value.astype(F32)
    give = total[CHUNK:].astype(BF16)
    got = chip_permute(give, 1)
    return total[:CHUNK] + got.astype(F32)


def near_reduce_scatter(part):
    blocks = part.reshape(4, 2, CHUNK, part.shape[1])
    got = chip_permute(blocks[:, 1].astype(BF16), 1)
    total = blocks[:, 0] + got.astype(F32)
    give = {k: total[k].astype(BF16) for k in (1, 3, 2)}
    got = [chip_permute(give[k], 2 * k) for k in (1, 3, 2)]
    total = total[0]
    for value in got:
        total = total + value.astype(F32)
    return total


def wide_reduce_scatter(part):
    half = part.shape[1] // 2
    first = near_reduce_scatter(part[:, :half])
    last = reduce_scatter(part[:, half:])
    return jnp.concatenate([first, last], axis=1)


def all_gather(block):
    pair = jnp.concatenate([block, chip_permute(block, 1)], axis=0)
    pairs = {k: chip_permute(pair, 2 * k) for k in (1, 3, 2)}
    return jnp.concatenate([pair, pairs[1], pairs[2], pairs[3]], axis=0)


def near_last_all_gather(block):
    quad = jnp.stack([block] + [chip_permute(block, 2 * k) for k in (1, 2, 3)])
    other = chip_permute(quad, 1)
    return jnp.stack([quad, other], axis=1).reshape(ROWS, block.shape[1])


def wide_all_gather(block):
    half = block.shape[1] // 2
    first = all_gather(block[:, :half])
    last = near_last_all_gather(block[:, half:])
    return jnp.concatenate([first, last], axis=1)


def all_reduce(part):
    half = part.shape[1] // 2
    first, last = part[:, :half], part[:, half:]
    first = first + row_permute(first.astype(BF16), 1).astype(F32)
    sent = last.astype(BF16)
    got = [row_permute(sent, k) for k in (2, 6, 4)]
    for value in got:
        last = last + value.astype(F32)
    sent = first.astype(BF16)
    got = [row_permute(sent, k) for k in (2, 6, 4)]
    for value in got:
        first = first + value.astype(F32)
    last = last + row_permute(last.astype(BF16), 1).astype(F32)
    return jnp.concatenate([first, last], axis=1)


def grads_kernel(core, left1, right1, left1_other, right1_other, left0, right0, left0_other, right0_other, out):
    pairs = ((left1, right1), (left1_other, right1_other), (left0, right0), (left0_other, right0_other))
    for step, (left, right) in enumerate(pairs):

        @pl.when(pl.program_id(0) == step)
        def _(left=left, right=right):
            out[0] = lax.dot_general(left[...], right[...], contract_rows, preferred_element_type=F32)


def weight_grads(core, operands, shape, axis):
    block = [1, shape[1], shape[2]]
    block[axis] //= 2

    def place(step, core):
        index = [1 - step // 2, 0, 0]
        index[axis] = (core[0] + step) % 2
        return tuple(index)

    return pl.pallas_call(
        grads_kernel,
        out_shape=jax.ShapeDtypeStruct(shape, F32),
        grid_spec=pltpu.PrefetchScalarGridSpec(
            num_scalar_prefetch=1,
            grid=(4,),
            in_specs=[pl.BlockSpec(value.shape, lambda step, core: (0, 0)) for value in operands],
            out_specs=pl.BlockSpec(tuple(block), place),
        ),
        compiler_params=pltpu.CompilerParams(vmem_limit_bytes=40 * 2**20),
    )(jnp.reshape(core, (1,)).astype(jnp.int32), *operands)


def gelu_both(pre):
    tangent = jnp.tanh(gelu_scale * (pre + cubic_term * pre * pre * pre))
    value = 0.5 * pre * (1.0 + tangent)
    slope = 0.5 * (1.0 + tangent) + 0.5 * pre * (1.0 - tangent * tangent) * gelu_scale * (
        1.0 + 3.0 * cubic_term * pre * pre
    )
    return value, slope


def dot(a, b):
    return jnp.dot(a, b, preferred_element_type=F32)


def pad_row(row, width):
    return jnp.pad(row, ((0, 0), (0, width - row.shape[1])))


def whole(tokens, counts, cotangent, up_weight, down_weight, norm_gain):
    core = lax.axis_index("col") % 2
    chip = lax.axis_index("col") // 2

    up_blocks, down_blocks, gains = [], [], []
    gain_other = swap_cores(norm_gain)
    for layer in range(2):
        keep = lax.dynamic_slice_in_dim(up_weight[layer], core * 1024, 1024, 1)
        give = lax.dynamic_slice_in_dim(up_weight[layer], (1 - core) * 1024, 1024, 1)
        up_blocks.append(jnp.concatenate([keep, swap_cores(give)], axis=0))
        keep = lax.dynamic_slice_in_dim(down_weight[layer], core * 1024, 1024, 0)
        give = lax.dynamic_slice_in_dim(down_weight[layer], (1 - core) * 1024, 1024, 0)
        down_blocks.append(jnp.concatenate([keep, swap_cores(give)], axis=1))
        gains.append(jnp.concatenate([norm_gain[layer], gain_other[layer]])[None, :])

    live = (jnp.arange(4, dtype=jnp.int32) < counts[0])[:, None]
    mixed = jnp.concatenate(
        [jnp.where(live, tokens, jnp.asarray(DEAD, BF16)), jnp.where(live, cotangent, jnp.asarray(0, BF16))], axis=0
    )
    mixed = mixed.reshape(8, 16, 256).transpose(1, 0, 2)
    mixed = jnp.broadcast_to(mixed[None], (8, 16, 8, 256)).reshape(128, 8, 256)
    mixed = lax.all_to_all(mixed, ("row", "col"), split_axis=0, concat_axis=0, tiled=True).reshape(1024, 256)

    pick = (lax.broadcasted_iota(jnp.int32, (8, 256), 1) == 0).astype(BF16)
    marks = lax.dot_general(pick, mixed, contract_cols, preferred_element_type=F32)[:1]
    lane = lax.broadcasted_iota(jnp.int32, (1, 1024), 1)
    alive = (marks < 1e20) & (lane % 8 < 4)
    before = lax.broadcasted_iota(jnp.int32, (1024, 1024), 0) < lax.broadcasted_iota(jnp.int32, (1024, 1024), 1)
    place = dot(jnp.broadcast_to(alive, (8, 1024)).astype(BF16), before.astype(BF16))[:1].astype(jnp.int32)
    place = ((place // LIVE_PER_CHUNK) ^ chip) * CHUNK + place % LIVE_PER_CHUNK
    place = jnp.where(alive, place, -1)
    slots = lax.broadcasted_iota(jnp.int32, (ROWS, 1024), 0)
    stream_own = dot((slots == place).astype(BF16), mixed).astype(BF16)
    place_grad = jnp.where(lane % 8 < 4, -1, jnp.roll(place, 4, axis=1))
    grad_own = dot((slots == place_grad).astype(BF16), mixed).astype(BF16)
    back = jnp.where(lane % 8 == 4, LIVE_PER_CHUNK, jnp.where(lane % 8 == 5, LIVE_PER_CHUNK + 1, place))
    back = (slots == back).astype(BF16).T

    line = lax.broadcasted_iota(jnp.int32, (ROWS, 1), 0)
    shared = ((line // CHUNK) ^ chip) * CHUNK + line % CHUNK
    seat = shared == lax.broadcasted_iota(jnp.int32, (ROWS, ROWS), 1)
    real_all = line % CHUNK < LIVE_PER_CHUNK
    real_own = real_all[:CHUNK]

    def to_row(column):
        return jnp.sum(jnp.where(seat[: column.shape[0]], column, 0.0), axis=0, keepdims=True)

    def to_column(row, rows):
        return jnp.sum(jnp.where(seat[:rows], row, 0.0), axis=1, keepdims=True)

    def both(own):
        return jnp.concatenate([own, swap_cores(own)], axis=1)

    def hidden_grad(grad_pair, layer):
        part = lax.dot_general(grad_pair, down_blocks[layer], contract_cols, preferred_element_type=F32)
        return reduce_scatter(part) if layer == 1 else wide_reduce_scatter(part)

    def fold_cores(pair):
        return pair[:, :256] + swap_cores(pair[:, 256:].astype(BF16)).astype(F32)

    grad_pair = both(grad_own)
    stream_pair = both(stream_own)
    grad_f32 = grad_own.astype(F32)

    saved = []
    for layer in range(2):
        scaled = (stream_pair.astype(F32) * gains[layer]).astype(BF16)
        squares = jnp.sum(jnp.square(stream_pair.astype(F32)), axis=1, keepdims=True)
        part = jnp.where(line % CHUNK == SIDE, pad_row(to_row(squares), 1024), dot(scaled, up_blocks[layer]))
        summed = wide_reduce_scatter(part)
        rstd = lax.rsqrt(summed[SIDE : SIDE + 1, :ROWS] / D + epsilon_norm)
        pre = jnp.where(real_own, summed * to_column(rstd, CHUNK), 0.0)
        value, slope = gelu_both(pre)
        hidden = value.astype(BF16)
        hidden = wide_all_gather(hidden) if layer == 0 else all_gather(hidden)
        saved.append((stream_own, stream_pair, to_column(rstd, ROWS), pre, slope, hidden))
        if layer == 0:
            moved = all_reduce(fold_cores(dot(hidden, down_blocks[0])))
            stream_own = (stream_own.astype(F32) + moved).astype(BF16)
            stream_pair = both(stream_own)

    up_operands, down_operands, gain_parts = [], [], [None, None]
    for layer in (1, 0):
        stream_own, stream_pair, rstd, pre, slope, hidden = saved[layer]
        grad_hidden = hidden_grad(grad_pair, layer)
        grad_pre = (grad_hidden * slope).astype(BF16)
        inner = to_row(jnp.sum(grad_pre.astype(F32) * pre, axis=1, keepdims=True))
        grad_pre = jnp.where(line[:CHUNK] == SIDE, pad_row(inner, 1024).astype(BF16), grad_pre)
        grad_pre = wide_all_gather(grad_pre)
        inner = jnp.sum(grad_pre.reshape(CHUNKS, CHUNK, 1024)[:, SIDE, :ROWS].astype(F32), axis=0, keepdims=True)
        inner = to_column(inner, ROWS)
        grad_normed = lax.dot_general(grad_pre, up_blocks[layer], contract_cols, preferred_element_type=F32)
        unit = stream_pair.astype(F32) * rstd
        gain_parts[layer] = jnp.sum(jnp.where(real_all, grad_normed * unit, 0.0), axis=0, keepdims=True)
        change = jnp.where(real_all, rstd * (grad_normed * gains[layer] - unit * (inner / D)), 0.0)
        if layer == 0:
            change = jnp.where(line == LIVE_PER_CHUNK, gain_parts[0], change)
            change = jnp.where(line == LIVE_PER_CHUNK + 1, gain_parts[1], change)
        change = fold_cores(change)

        unit_own = jnp.where(real_all, stream_own.astype(F32) * rstd * norm_gain[layer][None, :], 0.0).astype(BF16)
        up_operands += [unit_own, grad_pre, unit_own, swap_cores(grad_pre)]
        down_operands += [hidden, grad_own, swap_cores(hidden), grad_own]

        if layer == 1:
            grad_f32 = grad_f32 + all_reduce(change)
            grad_own = grad_f32.astype(BF16)
            grad_pair = both(grad_own)
        else:
            change = (change + 0.125 * grad_f32).astype(BF16)
            spread = dot(back, change).astype(BF16).reshape(128, 8, 256)
            spread = lax.all_to_all(spread, ("row", "col"), split_axis=0, concat_axis=0, tiled=True)
            summed = jnp.sum(spread.reshape(8, 16, 8, 256).astype(F32), axis=0)
            gain_grad = lax.dynamic_index_in_dim(summed, lax.axis_index("col"), 0, keepdims=False)[4:6]
            token_grad = summed[:, :4].astype(BF16).transpose(1, 0, 2).reshape(4, 4096)
    up_grads = weight_grads(core, up_operands, (2, 256, 2048), 2)
    down_grads = weight_grads(core, down_operands, (2, 2048, 256), 1)
    return token_grad, up_grads, down_grads, gain_grad


def solution(mesh):
    placed = (
        P(("row", "col"), None),
        P(("row", "col")),
        P(("row", "col"), None),
        P(None, "col", "row"),
        P(None, "row", "col"),
        P(None, "col"),
    )
    return jax.shard_map(
        whole,
        mesh=mesh,
        in_specs=placed,
        out_specs=(
            P(("row", "col"), None),
            P(None, "col", "row"),
            P(None, "row", "col"),
            P(None, "col"),
        ),
        check_vma=False,
    )
```

```python
import functools

import jax
import jax.numpy as jnp
from jax import lax
from jax.experimental import pallas as pl
from jax.experimental.pallas import tpu as pltpu
from jax.sharding import PartitionSpec as P


D = 4096
F32 = jnp.float32
BF16 = jnp.bfloat16

epsilon_norm = 1e-06
gelu_scale = 0.7978845608028654
cubic_term = 0.044715
contract_rows = (((0,), (0,)), ((), ()))
contract_cols = (((1,), (1,)), ((), ()))

LIVE_PER_CHUNK = 52
CHUNK = 56
CHUNKS = 8
ROWS = CHUNK * CHUNKS
SIDE = LIVE_PER_CHUNK
DEAD = 1e30


def swap_cores(value):
    return lax.ppermute(value, "col", [(i, i ^ 1) for i in range(16)])


def chip_permute(value, bits):
    return lax.ppermute(value, "col", [(i, i ^ (2 * bits)) for i in range(16)])


def row_permute(value, bits):
    return lax.ppermute(value, "row", [(i, i ^ bits) for i in range(8)])


def reduce_scatter(part):
    blocks = part.reshape(4, 2 * CHUNK, part.shape[1])
    got = [chip_permute(blocks[k].astype(BF16), 2 * k) for k in (1, 3, 2)]
    total = blocks[0]
    for value in got:
        total = total + value.astype(F32)
    give = total[CHUNK:].astype(BF16)
    got = chip_permute(give, 1)
    return total[:CHUNK] + got.astype(F32)


def near_reduce_scatter(part):
    blocks = part.reshape(4, 2, CHUNK, part.shape[1])
    got = chip_permute(blocks[:, 1].astype(BF16), 1)
    total = blocks[:, 0] + got.astype(F32)
    give = {k: total[k].astype(BF16) for k in (1, 3, 2)}
    got = [chip_permute(give[k], 2 * k) for k in (1, 3, 2)]
    total = total[0]
    for value in got:
        total = total + value.astype(F32)
    return total


def wide_reduce_scatter(part):
    half = part.shape[1] // 2
    first = near_reduce_scatter(part[:, :half])
    last = reduce_scatter(part[:, half:])
    return jnp.concatenate([first, last], axis=1)


def all_gather(block):
    pair = jnp.concatenate([block, chip_permute(block, 1)], axis=0)
    pairs = {k: chip_permute(pair, 2 * k) for k in (1, 3, 2)}
    return jnp.concatenate([pair, pairs[1], pairs[2], pairs[3]], axis=0)


def near_last_all_gather(block):
    quad = jnp.stack([block] + [chip_permute(block, 2 * k) for k in (1, 2, 3)])
    other = chip_permute(quad, 1)
    return jnp.stack([quad, other], axis=1).reshape(ROWS, block.shape[1])


def wide_all_gather(block):
    half = block.shape[1] // 2
    first = all_gather(block[:, :half])
    last = near_last_all_gather(block[:, half:])
    return jnp.concatenate([first, last], axis=1)


def all_reduce(part):
    half = part.shape[1] // 2
    first, last = part[:, :half], part[:, half:]
    first = first + row_permute(first.astype(BF16), 1).astype(F32)
    sent = last.astype(BF16)
    got = [row_permute(sent, k) for k in (2, 6, 4)]
    for value in got:
        last = last + value.astype(F32)
    sent = first.astype(BF16)
    got = [row_permute(sent, k) for k in (2, 6, 4)]
    for value in got:
        first = first + value.astype(F32)
    last = last + row_permute(last.astype(BF16), 1).astype(F32)
    return jnp.concatenate([first, last], axis=1)


def grads_kernel(axis, parts, core, *refs):
    operands, (out, small, large, sems) = refs[:6], refs[6:]
    step = pl.program_id(0)

    def copies(index, slot):
        layer, other = index // 2, index % 2
        source = operands[3 * layer + 1 + other]
        if other:
            source = source.at[pl.ds(parts[layer] * ROWS, ROWS)]
        return [
            pltpu.make_async_copy(operands[3 * layer], small.at[slot], sems.at[0, slot]),
            pltpu.make_async_copy(source, large.at[slot], sems.at[1, slot]),
        ]

    def fetch(wanted, slot):
        for index in range(4):

            @pl.when(wanted == index)
            def _(index=index):
                for copy in copies(index, slot):
                    copy.start()

    @pl.when(step == 0)
    def _():
        fetch(step, 0)

    slot = step % 2

    @pl.when(step < 3)
    def _():
        fetch(step + 1, 1 - slot)

    for copy in copies(0, slot):
        copy.wait()
    left, right = (small, large) if axis == 2 else (large, small)
    out[0] = lax.dot_general(left[slot], right[slot], contract_rows, preferred_element_type=F32)


def weight_grads(core, operands, shape, axis):
    block = [1, shape[1], shape[2]]
    block[axis] //= 2
    parts = (operands[2][1], operands[5][1])
    operands = [value[0] if isinstance(value, tuple) else value for value in operands]

    def place(step, core):
        index = [1 - step // 2, 0, 0]
        index[axis] = (core[0] + step) % 2
        return tuple(index)

    return pl.pallas_call(
        functools.partial(grads_kernel, axis, parts),
        out_shape=jax.ShapeDtypeStruct(shape, F32),
        grid_spec=pltpu.PrefetchScalarGridSpec(
            num_scalar_prefetch=1,
            grid=(4,),
            in_specs=[pl.BlockSpec(memory_space=pl.ANY)] * 6,
            out_specs=pl.BlockSpec(tuple(block), place),
            scratch_shapes=[
                pltpu.VMEM((2, ROWS, 256), BF16),
                pltpu.VMEM((2, ROWS, 1024), BF16),
                pltpu.SemaphoreType.DMA((2, 2)),
            ],
        ),
        compiler_params=pltpu.CompilerParams(vmem_limit_bytes=40 * 2**20),
    )(jnp.reshape(core, (1,)).astype(jnp.int32), *operands)


def gelu_both(pre):
    tangent = jnp.tanh(gelu_scale * (pre + cubic_term * pre * pre * pre))
    value = 0.5 * pre * (1.0 + tangent)
    slope = 0.5 * (1.0 + tangent) + 0.5 * pre * (1.0 - tangent * tangent) * gelu_scale * (
        1.0 + 3.0 * cubic_term * pre * pre
    )
    return value, slope


def dot(a, b):
    return jnp.dot(a, b, preferred_element_type=F32)


def pad_row(row, width):
    return jnp.pad(row, ((0, 0), (0, width - row.shape[1])))


def whole(tokens, counts, cotangent, up_weight, down_weight, norm_gain):
    core = lax.axis_index("col") % 2
    chip = lax.axis_index("col") // 2

    gain_other = swap_cores(norm_gain)
    up_other = swap_cores(lax.dynamic_slice_in_dim(up_weight, (1 - core) * 1024, 1024, 2))
    down_other = swap_cores(lax.dynamic_slice_in_dim(down_weight, (1 - core) * 1024, 1024, 1))
    up_keep = lax.dynamic_slice_in_dim(up_weight, core * 1024, 1024, 2)
    down_keep = lax.dynamic_slice_in_dim(down_weight, core * 1024, 1024, 1)
    up_blocks = [jnp.concatenate([up_keep[layer], up_other[layer]], axis=0) for layer in range(2)]
    down_blocks = [jnp.concatenate([down_keep[layer], down_other[layer]], axis=1) for layer in range(2)]
    gains = [jnp.concatenate([norm_gain[layer], gain_other[layer]])[None, :] for layer in range(2)]

    live = (jnp.arange(4, dtype=jnp.int32) < counts[0])[:, None]
    mixed = jnp.concatenate(
        [jnp.where(live, tokens, jnp.asarray(DEAD, BF16)), jnp.where(live, cotangent, jnp.asarray(0, BF16))], axis=0
    )
    mixed = mixed.reshape(8, 16, 256).transpose(1, 0, 2)
    mixed = jnp.broadcast_to(mixed[None], (8, 16, 8, 256)).reshape(128, 8, 256)
    mixed = lax.all_to_all(mixed, ("row", "col"), split_axis=0, concat_axis=0, tiled=True).reshape(1024, 256)

    pick = (lax.broadcasted_iota(jnp.int32, (8, 256), 1) == 0).astype(BF16)
    marks = lax.dot_general(pick, mixed, contract_cols, preferred_element_type=F32)[:1]
    lane = lax.broadcasted_iota(jnp.int32, (1, 1024), 1)
    alive = (marks < 1e20) & (lane % 8 < 4)
    before = lax.broadcasted_iota(jnp.int32, (1024, 1024), 0) < lax.broadcasted_iota(jnp.int32, (1024, 1024), 1)
    place = dot(jnp.broadcast_to(alive, (8, 1024)).astype(BF16), before.astype(BF16))[:1].astype(jnp.int32)
    place = ((place // LIVE_PER_CHUNK) ^ chip) * CHUNK + place % LIVE_PER_CHUNK
    place = jnp.where(alive, place, -1)
    slots = lax.broadcasted_iota(jnp.int32, (ROWS, 1024), 0)
    place_grad = jnp.where(lane % 8 < 4, -1, jnp.roll(place, 4, axis=1))
    chosen = jnp.concatenate([slots == place, slots == place_grad], axis=0).astype(BF16)
    packed = dot(chosen, mixed).astype(BF16)
    stream_own, grad_own = packed[:ROWS], packed[ROWS:]
    packed_other = swap_cores(packed)
    back = jnp.where(lane % 8 == 4, LIVE_PER_CHUNK, jnp.where(lane % 8 == 5, LIVE_PER_CHUNK + 1, place))
    back = (slots == back).astype(BF16).T

    line = lax.broadcasted_iota(jnp.int32, (ROWS, 1), 0)
    shared = ((line // CHUNK) ^ chip) * CHUNK + line % CHUNK
    seat = shared == lax.broadcasted_iota(jnp.int32, (ROWS, ROWS), 1)
    real_all = line % CHUNK < LIVE_PER_CHUNK
    real_own = real_all[:CHUNK]

    def to_row(column):
        return jnp.sum(jnp.where(seat[: column.shape[0]], column, 0.0), axis=0, keepdims=True)

    def to_column(row, rows):
        return jnp.sum(jnp.where(seat[:rows], row, 0.0), axis=1, keepdims=True)

    def both(own):
        return jnp.concatenate([own, swap_cores(own)], axis=1)

    def hidden_grad(grad_pair, layer):
        part = lax.dot_general(grad_pair, down_blocks[layer], contract_cols, preferred_element_type=F32)
        return reduce_scatter(part) if layer == 1 else wide_reduce_scatter(part)

    def fold_cores(pair):
        return pair[:, :256] + swap_cores(pair[:, 256:].astype(BF16)).astype(F32)

    stream_pair = jnp.concatenate([stream_own, packed_other[:ROWS]], axis=1)
    grad_pair = jnp.concatenate([grad_own, packed_other[ROWS:]], axis=1)
    grad_f32 = grad_own.astype(F32)

    saved = []
    for layer in range(2):
        scaled = (stream_pair.astype(F32) * gains[layer]).astype(BF16)
        squares = jnp.sum(jnp.square(stream_pair.astype(F32)), axis=1, keepdims=True)
        part = jnp.where(line % CHUNK == SIDE, pad_row(to_row(squares), 1024), dot(scaled, up_blocks[layer]))
        summed = wide_reduce_scatter(part)
        rstd = lax.rsqrt(summed[SIDE : SIDE + 1, :ROWS] / D + epsilon_norm)
        pre = jnp.where(real_own, summed * to_column(rstd, CHUNK), 0.0)
        value, slope = gelu_both(pre)
        hidden = value.astype(BF16)
        hidden = wide_all_gather(hidden) if layer == 0 else all_gather(hidden)
        saved.append((stream_own, stream_pair, to_column(rstd, ROWS), pre, slope, hidden))
        if layer == 0:
            moved = all_reduce(fold_cores(dot(hidden, down_blocks[0])))
            stream_own = (stream_own.astype(F32) + moved).astype(BF16)
            stream_pair = both(stream_own)

    gain_parts, units, grad_pres, grads, hiddens = ([None, None] for _ in range(5))
    for layer in (1, 0):
        stream_own, stream_pair, rstd, pre, slope, hidden = saved[layer]
        grad_hidden = hidden_grad(grad_pair, layer)
        grad_pre = (grad_hidden * slope).astype(BF16)
        inner = to_row(jnp.sum(grad_pre.astype(F32) * pre, axis=1, keepdims=True))
        grad_pre = jnp.where(line[:CHUNK] == SIDE, pad_row(inner, 1024).astype(BF16), grad_pre)
        grad_pre = wide_all_gather(grad_pre)
        inner = jnp.sum(grad_pre.reshape(CHUNKS, CHUNK, 1024)[:, SIDE, :ROWS].astype(F32), axis=0, keepdims=True)
        inner = to_column(inner, ROWS)
        grad_normed = lax.dot_general(grad_pre, up_blocks[layer], contract_cols, preferred_element_type=F32)
        unit = stream_pair.astype(F32) * rstd
        gain_parts[layer] = jnp.sum(jnp.where(real_all, grad_normed * unit, 0.0), axis=0, keepdims=True)
        change = jnp.where(real_all, rstd * (grad_normed * gains[layer] - unit * (inner / D)), 0.0)
        if layer == 0:
            change = jnp.where(line == LIVE_PER_CHUNK, gain_parts[0], change)
            change = jnp.where(line == LIVE_PER_CHUNK + 1, gain_parts[1], change)
        change = fold_cores(change)

        unit_own = jnp.where(real_all, stream_own.astype(F32) * rstd * norm_gain[layer][None, :], 0.0).astype(BF16)
        units[layer], grad_pres[layer], grads[layer], hiddens[layer] = unit_own, grad_pre, grad_own, hidden

        if layer == 1:
            grad_f32 = grad_f32 + all_reduce(change)
            grad_own = grad_f32.astype(BF16)
            grad_pair = both(grad_own)
        else:
            change = (change + 0.125 * grad_f32).astype(BF16)
            spread = dot(back, change).astype(BF16).reshape(128, 8, 256)
            spread = lax.all_to_all(spread, ("row", "col"), split_axis=0, concat_axis=0, tiled=True)
            summed = jnp.sum(spread.reshape(8, 16, 8, 256).astype(F32), axis=0)
            gain_grad = lax.dynamic_index_in_dim(summed, lax.axis_index("col"), 0, keepdims=False)[4:6]
            token_grad = summed[:, :4].astype(BF16).transpose(1, 0, 2).reshape(4, 4096)
    early = swap_cores(jnp.concatenate([hiddens[0], hiddens[1], grad_pres[1]], axis=0))
    late = swap_cores(grad_pres[0])
    operands = (units[1], grad_pres[1], (early, 2), units[0], grad_pres[0], (late, 0))
    up_grads = weight_grads(core, operands, (2, 256, 2048), 2)
    operands = (grads[1], hiddens[1], (early, 1), grads[0], hiddens[0], (early, 0))
    down_grads = weight_grads(core, operands, (2, 2048, 256), 1)
    return token_grad, up_grads, down_grads, gain_grad


def solution(mesh):
    placed = (
        P(("row", "col"), None),
        P(("row", "col")),
        P(("row", "col"), None),
        P(None, "col", "row"),
        P(None, "row", "col"),
        P(None, "col"),
    )
    return jax.shard_map(
        whole,
        mesh=mesh,
        in_specs=placed,
        out_specs=(
            P(("row", "col"), None),
            P(None, "col", "row"),
            P(None, "row", "col"),
            P(None, "col"),
        ),
        check_vma=False,
    )
```

```python
import functools

import jax
import jax.numpy as jnp
from jax import lax
from jax.experimental import pallas as pl
from jax.experimental.pallas import tpu as pltpu
from jax.sharding import PartitionSpec as P


D = 4096
F32 = jnp.float32
BF16 = jnp.bfloat16

epsilon_norm = 1e-06
gelu_scale = 0.7978845608028654
cubic_term = 0.044715
contract_rows = (((0,), (0,)), ((), ()))
contract_cols = (((1,), (1,)), ((), ()))

LIVE_PER_CHUNK = 52
CHUNK = 56
CHUNKS = 8
ROWS = CHUNK * CHUNKS
SIDE = LIVE_PER_CHUNK
DEAD = 1e30


def swap_cores(value):
    return lax.ppermute(value, "col", [(i, i ^ 1) for i in range(16)])


def chip_permute(value, bits):
    return lax.ppermute(value, "col", [(i, i ^ (2 * bits)) for i in range(16)])


def row_permute(value, bits):
    return lax.ppermute(value, "row", [(i, i ^ bits) for i in range(8)])


def reduce_scatter(part):
    blocks = part.reshape(4, 2 * CHUNK, part.shape[1])
    got = [chip_permute(blocks[k].astype(BF16), 2 * k) for k in (1, 3, 2)]
    total = blocks[0]
    for value in got:
        total = total + value.astype(F32)
    give = total[CHUNK:].astype(BF16)
    got = chip_permute(give, 1)
    return total[:CHUNK] + got.astype(F32)


def near_reduce_scatter(part):
    blocks = part.reshape(4, 2, CHUNK, part.shape[1])
    got = chip_permute(blocks[:, 1].astype(BF16), 1)
    total = blocks[:, 0] + got.astype(F32)
    give = {k: total[k].astype(BF16) for k in (1, 3, 2)}
    got = [chip_permute(give[k], 2 * k) for k in (1, 3, 2)]
    total = total[0]
    for value in got:
        total = total + value.astype(F32)
    return total


def wide_reduce_scatter(part):
    half = part.shape[1] // 2
    first = near_reduce_scatter(part[:, :half])
    last = reduce_scatter(part[:, half:])
    return jnp.concatenate([first, last], axis=1)


def all_gather(block):
    pair = jnp.concatenate([block, chip_permute(block, 1)], axis=0)
    pairs = {k: chip_permute(pair, 2 * k) for k in (1, 3, 2)}
    return jnp.concatenate([pair, pairs[1], pairs[2], pairs[3]], axis=0)


def near_last_all_gather(block):
    quad = jnp.stack([block] + [chip_permute(block, 2 * k) for k in (1, 2, 3)])
    other = chip_permute(quad, 1)
    return jnp.stack([quad, other], axis=1).reshape(ROWS, block.shape[1])


def wide_all_gather(block):
    half = block.shape[1] // 2
    first = all_gather(block[:, :half])
    last = near_last_all_gather(block[:, half:])
    return jnp.concatenate([first, last], axis=1)


def all_reduce(part):
    half = part.shape[1] // 2
    first, last = part[:, :half], part[:, half:]
    first = first + row_permute(first.astype(BF16), 1).astype(F32)
    sent = last.astype(BF16)
    got = [row_permute(sent, k) for k in (2, 6, 4)]
    for value in got:
        last = last + value.astype(F32)
    sent = first.astype(BF16)
    got = [row_permute(sent, k) for k in (2, 6, 4)]
    for value in got:
        first = first + value.astype(F32)
    last = last + row_permute(last.astype(BF16), 1).astype(F32)
    return jnp.concatenate([first, last], axis=1)


def grads_kernel(axis, parts, core, *refs):
    operands, (out, small, large, sems) = refs[:6], refs[6:]
    step = pl.program_id(0)

    def copies(index, slot):
        layer, other = index // 2, index % 2
        source = operands[3 * layer + 1 + other]
        if other:
            source = source.at[pl.ds(parts[layer] * ROWS, ROWS)]
        return [
            pltpu.make_async_copy(operands[3 * layer], small.at[slot], sems.at[0, slot]),
            pltpu.make_async_copy(source, large.at[slot], sems.at[1, slot]),
        ]

    def fetch(wanted, slot):
        for index in range(4):

            @pl.when(wanted == index)
            def _(index=index):
                for copy in copies(index, slot):
                    copy.start()

    @pl.when(step == 0)
    def _():
        fetch(step, 0)

    slot = step % 2

    @pl.when(step < 3)
    def _():
        fetch(step + 1, 1 - slot)

    for copy in copies(0, slot):
        copy.wait()
    left, right = (small, large) if axis == 2 else (large, small)
    out[0] = lax.dot_general(left[slot], right[slot], contract_rows, preferred_element_type=F32)


def weight_grads(core, operands, shape, axis):
    block = [1, shape[1], shape[2]]
    block[axis] //= 2
    parts = (operands[2][1], operands[5][1])
    operands = [value[0] if isinstance(value, tuple) else value for value in operands]

    def place(step, core):
        index = [1 - step // 2, 0, 0]
        index[axis] = (core[0] + step) % 2
        return tuple(index)

    return pl.pallas_call(
        functools.partial(grads_kernel, axis, parts),
        out_shape=jax.ShapeDtypeStruct(shape, F32),
        grid_spec=pltpu.PrefetchScalarGridSpec(
            num_scalar_prefetch=1,
            grid=(4,),
            in_specs=[pl.BlockSpec(memory_space=pl.ANY)] * 6,
            out_specs=pl.BlockSpec(tuple(block), place),
            scratch_shapes=[
                pltpu.VMEM((2, ROWS, 256), BF16),
                pltpu.VMEM((2, ROWS, 1024), BF16),
                pltpu.SemaphoreType.DMA((2, 2)),
            ],
        ),
        compiler_params=pltpu.CompilerParams(vmem_limit_bytes=40 * 2**20),
    )(jnp.reshape(core, (1,)).astype(jnp.int32), *operands)


def gelu_both(pre):
    tangent = jnp.tanh(gelu_scale * (pre + cubic_term * pre * pre * pre))
    value = 0.5 * pre * (1.0 + tangent)
    slope = 0.5 * (1.0 + tangent) + 0.5 * pre * (1.0 - tangent * tangent) * gelu_scale * (
        1.0 + 3.0 * cubic_term * pre * pre
    )
    return value, slope


def dot(a, b):
    return jnp.dot(a, b, preferred_element_type=F32)


def pad_row(row, width):
    return jnp.pad(row, ((0, 0), (0, width - row.shape[1])))


def whole(tokens, counts, cotangent, up_weight, down_weight, norm_gain):
    core = lax.axis_index("col") % 2
    chip = lax.axis_index("col") // 2

    gain_other = swap_cores(norm_gain)
    up_other = swap_cores(lax.dynamic_slice_in_dim(up_weight, (1 - core) * 1024, 1024, 2))
    down_other = swap_cores(lax.dynamic_slice_in_dim(down_weight, (1 - core) * 1024, 1024, 1))
    up_keep = lax.dynamic_slice_in_dim(up_weight, core * 1024, 1024, 2)
    down_keep = lax.dynamic_slice_in_dim(down_weight, core * 1024, 1024, 1)
    up_blocks = [jnp.concatenate([up_keep[layer], up_other[layer]], axis=0) for layer in range(2)]
    down_blocks = [jnp.concatenate([down_keep[layer], down_other[layer]], axis=1) for layer in range(2)]
    gains = [jnp.concatenate([norm_gain[layer], gain_other[layer]])[None, :] for layer in range(2)]

    live = (jnp.arange(4, dtype=jnp.int32) < counts[0])[:, None]
    mixed = jnp.concatenate(
        [jnp.where(live, tokens, jnp.asarray(DEAD, BF16)), jnp.where(live, cotangent, jnp.asarray(0, BF16))], axis=0
    )
    mixed = mixed.reshape(8, 16, 256).transpose(1, 0, 2)
    mixed = jnp.broadcast_to(mixed[None], (8, 16, 8, 256)).reshape(128, 8, 256)
    mixed = lax.all_to_all(mixed, ("row", "col"), split_axis=0, concat_axis=0, tiled=True).reshape(1024, 256)

    pick = (lax.broadcasted_iota(jnp.int32, (8, 256), 1) == 0).astype(BF16)
    marks = lax.dot_general(pick, mixed, contract_cols, preferred_element_type=F32)[:1]
    lane = lax.broadcasted_iota(jnp.int32, (1, 1024), 1)
    alive = (marks < 1e20) & (lane % 8 < 4)
    before = lax.broadcasted_iota(jnp.int32, (1024, 1024), 0) < lax.broadcasted_iota(jnp.int32, (1024, 1024), 1)
    place = dot(jnp.broadcast_to(alive, (8, 1024)).astype(BF16), before.astype(BF16))[:1].astype(jnp.int32)
    place = ((place // LIVE_PER_CHUNK) ^ chip) * CHUNK + place % LIVE_PER_CHUNK
    place = jnp.where(alive, place, -1)
    slots = lax.broadcasted_iota(jnp.int32, (ROWS, 1024), 0)
    place_grad = jnp.where(lane % 8 < 4, -1, jnp.roll(place, 4, axis=1))
    chosen = jnp.concatenate([slots == place, slots == place_grad], axis=0).astype(BF16)
    packed = dot(chosen, mixed).astype(BF16)
    stream_own, grad_own = packed[:ROWS], packed[ROWS:]
    packed_other = swap_cores(packed)
    back = jnp.where(lane % 8 == 4, LIVE_PER_CHUNK, jnp.where(lane % 8 == 5, LIVE_PER_CHUNK + 1, place))
    back = (slots == back).astype(BF16).T

    line = lax.broadcasted_iota(jnp.int32, (ROWS, 1), 0)
    shared = ((line // CHUNK) ^ chip) * CHUNK + line % CHUNK
    seat = shared == lax.broadcasted_iota(jnp.int32, (ROWS, ROWS), 1)
    real_all = line % CHUNK < LIVE_PER_CHUNK
    real_own = real_all[:CHUNK]

    def to_row(column):
        return jnp.sum(jnp.where(seat[: column.shape[0]], column, 0.0), axis=0, keepdims=True)

    def to_column(row, rows):
        return jnp.sum(jnp.where(seat[:rows], row, 0.0), axis=1, keepdims=True)

    def both(own):
        return jnp.concatenate([own, swap_cores(own)], axis=1)

    def hidden_grad(grad_pair, layer):
        part = lax.dot_general(grad_pair, down_blocks[layer], contract_cols, preferred_element_type=F32)
        return reduce_scatter(part) if layer == 1 else wide_reduce_scatter(part)

    def fold_cores(pair):
        return pair[:, :256] + swap_cores(pair[:, 256:].astype(BF16)).astype(F32)

    stream_pair = jnp.concatenate([stream_own, packed_other[:ROWS]], axis=1)
    grad_pair = jnp.concatenate([grad_own, packed_other[ROWS:]], axis=1)
    grad_f32 = grad_own.astype(F32)

    saved = []
    for layer in range(2):
        scaled = (stream_pair.astype(F32) * gains[layer]).astype(BF16)
        squares = jnp.sum(jnp.square(stream_pair.astype(F32)), axis=1, keepdims=True)
        part = jnp.where(line % CHUNK == SIDE, pad_row(to_row(squares), 1024), dot(scaled, up_blocks[layer]))
        summed = wide_reduce_scatter(part)
        rstd = lax.rsqrt(summed[SIDE : SIDE + 1, :ROWS] / D + epsilon_norm)
        pre = jnp.where(real_own, summed * to_column(rstd, CHUNK), 0.0)
        value, slope = gelu_both(pre)
        hidden = value.astype(BF16)
        hidden = wide_all_gather(hidden) if layer == 0 else all_gather(hidden)
        saved.append((stream_own, stream_pair, to_column(rstd, ROWS), pre, slope, hidden))
        if layer == 0:
            moved = all_reduce(fold_cores(dot(hidden, down_blocks[0])))
            stream_own = (stream_own.astype(F32) + moved).astype(BF16)
            stream_pair = both(stream_own)

    gain_parts, units, grad_pres, grads, hiddens = ([None, None] for _ in range(5))
    for layer in (1, 0):
        stream_own, stream_pair, rstd, pre, slope, hidden = saved[layer]
        grad_hidden = hidden_grad(grad_pair, layer)
        grad_pre = (grad_hidden * slope).astype(BF16)
        inner = to_row(jnp.sum(grad_pre.astype(F32) * pre, axis=1, keepdims=True))
        grad_pre = jnp.where(line[:CHUNK] == SIDE, pad_row(inner, 1024).astype(BF16), grad_pre)
        grad_pre = wide_all_gather(grad_pre)
        inner = jnp.sum(grad_pre.reshape(CHUNKS, CHUNK, 1024)[:, SIDE, :ROWS].astype(F32), axis=0, keepdims=True)
        inner = to_column(inner, ROWS)
        grad_normed = lax.dot_general(grad_pre, up_blocks[layer], contract_cols, preferred_element_type=F32)
        unit = stream_pair.astype(F32) * rstd
        gain_parts[layer] = jnp.sum(jnp.where(real_all, grad_normed * unit, 0.0), axis=0, keepdims=True)
        change = jnp.where(real_all, rstd * (grad_normed * gains[layer] - unit * (inner / D)), 0.0)
        if layer == 0:
            change = jnp.where(line == LIVE_PER_CHUNK, gain_parts[0], change)
            change = jnp.where(line == LIVE_PER_CHUNK + 1, gain_parts[1], change)
        change = fold_cores(change)

        unit_own = jnp.where(real_all, stream_own.astype(F32) * rstd * norm_gain[layer][None, :], 0.0).astype(BF16)
        units[layer], grad_pres[layer], grads[layer], hiddens[layer] = unit_own, grad_pre, grad_own, hidden

        if layer == 1:
            grad_f32 = grad_f32 + all_reduce(change)
            grad_own = grad_f32.astype(BF16)
            grad_pair = both(grad_own)
        else:
            change = (change + 0.125 * grad_f32).astype(BF16)
            spread = dot(back, change).astype(BF16).reshape(128, 8, 256)
            spread = lax.all_to_all(spread, ("row", "col"), split_axis=0, concat_axis=0, tiled=True)
            summed = jnp.sum(spread.reshape(8, 16, 8, 256).astype(F32), axis=0)
            gain_grad = lax.dynamic_index_in_dim(summed, lax.axis_index("col"), 0, keepdims=False)[4:6]
            token_grad = summed[:, :4].astype(BF16).transpose(1, 0, 2).reshape(4, 4096)
    early, late = swap_cores(grad_pres[1]), swap_cores(grad_pres[0])
    hidden_others = [swap_cores(value) for value in hiddens]
    operands = (units[1], grad_pres[1], (early, 0), units[0], grad_pres[0], (late, 0))
    up_grads = weight_grads(core, operands, (2, 256, 2048), 2)
    operands = (grads[1], hiddens[1], (hidden_others[1], 0), grads[0], hiddens[0], (hidden_others[0], 0))
    down_grads = weight_grads(core, operands, (2, 2048, 256), 1)
    return token_grad, up_grads, down_grads, gain_grad


def solution(mesh):
    placed = (
        P(("row", "col"), None),
        P(("row", "col")),
        P(("row", "col"), None),
        P(None, "col", "row"),
        P(None, "row", "col"),
        P(None, "col"),
    )
    return jax.shard_map(
        whole,
        mesh=mesh,
        in_specs=placed,
        out_specs=(
            P(("row", "col"), None),
            P(None, "col", "row"),
            P(None, "row", "col"),
            P(None, "col"),
        ),
        check_vma=False,
    )
```
